256 devices in a mesh: rows: 64 (over x_hi, z, y), outs: 4 (over x_lo, core).
Axes of the slice: x: 4 (x_hi: 2, x_lo: 2; x = x_hi * 2 + x_lo), y: 4, z: 8, core: 2. Of those that a mesh axis runs over, the one named last changes fastest.
Arguments:
- grads: bfloat16 [393216, 1024], P('rows', 'outs'), may hold values from -6 to 6
- projection: bfloat16 [1024, 8], replicated, may hold values from -0.1875 to 0.1875
- bins: int32 [393216, 256], P('rows'), may hold values from 0 to 127
- leaf: int32 [393216], P('rows'), may hold values from 0 to 3
Outputs:
- histogram: float32 [64, 4, 4, 8, 128], P('rows', 'outs')
The draws below stay inside these ranges and needn't reach their ends.
All inputs are finite; a program needn't handle non-finite values.
Results may differ from the reference program's by a relative error of at most 0.0029.
Values may be sent and summed in bfloat16 or wider, within the bound.
A program may use at most 64 MiB of HBM per device.

```python
import math
import jax
import jax.numpy as jnp
from jax import lax

OUTW = 1024
SK = 8
FEATURES = 256
BINS = 128
LEAVES = 4
ROWS = 393216
FB = 64


def place_ends(entries, own_key, least, largest):
    spot = [jax.random.randint(jax.random.fold_in(own_key, axis), (), 0, length) for axis, length in enumerate(entries.shape)]
    widest = entries.shape.index(max(entries.shape))
    beside = spot[:widest] + [(spot[widest] + 1) % entries.shape[widest]] + spot[widest + 1:]
    return entries.at[tuple(spot)].set(least).at[tuple(beside)].set(largest)


def block_levels(own_key, shape, cuts, low, top_value):
    gain = 1.0
    for axis_at, blocks in cuts:
        heights = jax.random.uniform(jax.random.fold_in(jax.random.fold_in(own_key, 6), axis_at), (blocks,), jnp.float32, low / len(cuts), top_value / len(cuts))
        gain = gain * jnp.repeat(jnp.exp(heights), shape[axis_at] // blocks).reshape((-1,) + (1,) * (len(shape) - 1 - axis_at))
    return gain


def bell_draw(rng, dims, spread, limit, cuts=(), kind=jnp.bfloat16):
    result = jax.random.normal(rng, dims, jnp.float32) * spread
    if len(cuts) > 0:
        result = block_levels(rng, dims, cuts, -0.22, 0.18) * result
    return jnp.clip(result, min=-limit, max=limit).astype(kind)


def setup_inputs(seed: int = 0) -> dict:
    splits = jax.random.split(jax.random.key(seed), 5)
    grads = bell_draw(splits[0], (ROWS, OUTW), 1.0, 6.0, ((0, 64), (1, 4)))
    projection = bell_draw(splits[1], (OUTW, SK), OUTW ** -0.5, 0.1875)
    bins = place_ends(jax.random.randint(splits[2], (ROWS, FEATURES), 0, BINS), jax.random.fold_in(splits[2], 1), 0, BINS - 1).astype(jnp.int32)
    leaf = place_ends(jax.random.randint(splits[3], (ROWS,), 0, LEAVES), jax.random.fold_in(splits[3], 1), 0, LEAVES - 1).astype(jnp.int32)
    return dict(grads=grads, projection=projection, bins=bins, leaf=leaf)


def reference(grads, projection, bins, leaf):
    sketch = jnp.dot(grads, projection, preferred_element_type=jnp.float32).astype(jnp.bfloat16)
    leaf_hot = jax.nn.one_hot(leaf, LEAVES, dtype=jnp.float32)
    weights = (leaf_hot[:, :, None] * sketch.astype(jnp.float32)[:, None, :]).reshape(ROWS, LEAVES * SK)

    def one_feature(column):
        return jax.ops.segment_sum(weights, column, num_segments=BINS)
    sums = lax.map(one_feature, bins.T)
    sums = jnp.transpose(sums, (0, 2, 1)).reshape(FEATURES, LEAVES, SK, BINS)
    scaled = sums * jnp.float32(math.sqrt(LEAVES * BINS / ROWS))
    return jnp.transpose(scaled.reshape(FEATURES // FB, FB, LEAVES, SK, BINS), (1, 0, 2, 3, 4))
```

```python
import functools
import math

import jax
import jax.numpy as jnp
from jax import lax
from jax.experimental import pallas as pl
from jax.experimental.pallas import tpu as pltpu
from jax.sharding import PartitionSpec as P

SK = 8
BINS = 128
LEAVES = 4
MESH = pl.DeviceIdType.MESH
BF = jnp.bfloat16
F32 = jnp.float32
NX, NZ, NY, NO = 2, 8, 4, 4
STEPS = NX * NZ
LAG = 2


def pieces(n_rows):
    r = lax.axis_index("rows")
    return r // (NZ * NY), (r // NY) % NZ, r % NY


def kernel(
    scale,
    grads, proj, bins, leaf,
    out,
    gbuf, pbuf, bbuf, lbuf, part, skin, skq, skr, sk16, bh, cc,
    fbuf, sbuf, rbuf1, s2, rbuf2,
    lsem, osem, qs_send, qs_recv, ag_send, ag_recv, y_send, y_recv, z_send, z_recv,
):
    x, z, y = pieces(NX * NZ * NY)
    o = lax.axis_index("outs")
    rows = bh.shape[1]
    quarter = rows // NO
    half = quarter // 2
    order = (2, 1, 3, 0)

    pcopy = pltpu.make_async_copy(proj, pbuf, lsem.at[8])
    pcopy.start()
    gcopies = []
    for i, d in enumerate(order):
        q = (o + d) % NO
        g = pltpu.make_async_copy(
            grads.at[pl.ds(pl.multiple_of(q * quarter, quarter), quarter), :], gbuf.at[i], lsem.at[i]
        )
        g.start()
        gcopies.append(g)
    lcopy = pltpu.make_async_copy(leaf, lbuf, lsem.at[9])
    lcopy.start()
    bcopies = []
    for i in range(4):
        b = pltpu.make_async_copy(
            bins.at[pl.ds(i * quarter, quarter), pl.ds(pl.multiple_of((o // 2) * 128, 128), 128)],
            bbuf.at[pl.ds(i * quarter, quarter), :],
            lsem.at[4 + i],
        )
        b.start()
        bcopies.append(b)

    def row_id(xx, zz, yy):
        return xx * (NZ * NY) + zz * NY + yy

    def target(delta):
        return row_id((x + delta // NZ) % NX, (z + delta % NZ) % NZ, y)

    here = row_id(x, z, y)
    barrier = pltpu.get_barrier_semaphore()
    for d in range(1, NO):
        pl.semaphore_signal(barrier, inc=1, device_id=(here, (o + d) % NO), device_id_type=MESH)
    for d in range(1, NY):
        pl.semaphore_signal(barrier, inc=1, device_id=(row_id(x, z, (y + d) % NY), o), device_id_type=MESH)

    def greet(delta, carry):
        pl.semaphore_signal(barrier, inc=1, device_id=(target(delta), o), device_id_type=MESH)
        return carry

    lax.fori_loop(1, STEPS, greet, 0)

    pcopy.wait()
    pmat = pbuf[pl.ds(pl.multiple_of(o * 256, 256), 256), :]

    def quarter_copy(i, d):
        return pltpu.make_async_remote_copy(
            src_ref=part.at[i], dst_ref=skin.at[d - 1], send_sem=qs_send.at[d - 1], recv_sem=qs_recv.at[d - 1],
            device_id=(here, (o + d) % NO), device_id_type=MESH,
        )

    for i, d in enumerate(order):
        gcopies[i].wait()
        part[i] = lax.dot_general(pmat, gbuf[i], (((0,), (1,)), ((), ())), preferred_element_type=F32)
        if i == 0:
            pl.semaphore_wait(barrier, (NO - 1) + (NY - 1) + (STEPS - 1))
        if d:
            quarter_copy(i, d).start()

    lcopy.wait()
    own_col = lax.broadcasted_iota(jnp.int32, (64, 128), 1) - (o % 2) * 64
    pick = (own_col == lax.broadcasted_iota(jnp.int32, (64, 128), 0)).astype(F32).astype(BF)

    def turn(i):
        bcopies[i].wait()
        block = bbuf[pl.ds(i * quarter, quarter), :].astype(F32).astype(BF)
        b = lax.dot_general(pick, block, (((1,), (1,)), ((), ())), preferred_element_type=F32)
        high = jnp.floor(b * F32(1.0 / 16.0))
        low = b - high * F32(16.0)
        lanes = pl.ds(i * quarter, quarter)
        bh[:, lanes] = high
        tiles = quarter // 128
        for t in range(tiles):
            leaf_row = lbuf[pl.ds(i * tiles + t, 1), :].astype(F32) * F32(16.0)
            cc[:, pl.ds(i * quarter + t * 128, 128)] = low[:, t * 128:(t + 1) * 128] + leaf_row

    turn(0)
    turn(1)
    for d in range(1, NO):
        quarter_copy(0, d).wait_recv()
    mine = ((part[3] + skin[0]) + (skin[1] + skin[2]))
    skq[...] = jnp.concatenate([mine[:, :half], mine[:, half:]], 0).astype(BF)

    def gather_copy(d):
        return pltpu.make_async_remote_copy(
            src_ref=skq, dst_ref=skr.at[d - 1], send_sem=ag_send.at[d - 1], recv_sem=ag_recv.at[d - 1],
            device_id=(here, (o + d) % NO), device_id_type=MESH,
        )

    for d in (2, 1, 3):
        gather_copy(d).start()
    turn(2)
    turn(3)

    def spread(packed, owner):
        wide = packed.astype(F32)
        for h in range(2):
            rows8 = wide[8 * h:8 * h + 8]
            sk16[:, pl.ds(pl.multiple_of(owner * quarter + h * half, half), half)] = jnp.concatenate(
                [rows8, rows8], 0
            ).astype(BF)

    spread(skq[...], o)
    for d in range(1, NO):
        gather_copy(d).wait_recv()
        spread(skr[d - 1], (o + NO - d) % NO)

    sub16 = lax.broadcasted_iota(jnp.int32, (16, rows), 0)
    pair = (sub16 // 8).astype(F32).astype(BF)
    sixteen = sub16.astype(F32).astype(BF)
    lane = lax.broadcasted_iota(jnp.int32, (32, 128), 1)

    def y_copy(t, d):
        to = (y + d) % NY
        return pltpu.make_async_remote_copy(
            src_ref=sbuf.at[t, to], dst_ref=rbuf1.at[t, d - 1], send_sem=y_send.at[t, d - 1],
            recv_sem=y_recv.at[t, d - 1], device_id=(row_id(x, z, to), o), device_id_type=MESH,
        )

    def z_copy(t):
        return pltpu.make_async_remote_copy(
            src_ref=s2.at[t], dst_ref=rbuf2.at[t], send_sem=z_send.at[t], recv_sem=z_recv.at[t],
            device_id=(target(STEPS - 1 - t), o), device_id_type=MESH,
        )

    def gather_y(t):
        for d in range(1, NY):
            y_copy(t, d).wait_recv()
        return (fbuf[t, y] + rbuf1[t, 0].astype(F32)) + (rbuf1[t, 1].astype(F32) + rbuf1[t, 2].astype(F32))

    def send_on(t):
        s2[t] = gather_y(t)
        z_copy(t).start()

    def step(t, carry):
        delta = STEPS - 1 - t
        base = (((x + delta // NZ) % NX) * NZ + (z + delta % NZ) % NZ) * NY
        weights = sk16[...]
        left, right = [], []
        for f in range(NY):
            b16 = jnp.broadcast_to(bh[pl.ds(base + f, 1), :], (16, rows)).astype(BF)
            c16 = jnp.broadcast_to(cc[pl.ds(base + f, 1), :], (16, rows)).astype(BF)
            for m in range(4):
                left.append(jnp.where(b16 == pair + BF(2 * m), weights, BF(0)))
            for m in range(4):
                right.append(jnp.where(c16 == sixteen + BF(16 * m), BF(1), BF(0)))
        both = lax.dot_general(
            jnp.concatenate(left, 0), jnp.concatenate(right, 0), (((1,), (1,)), ((), ())),
            preferred_element_type=F32,
        )
        for f in range(NY):
            block = both[f * 64:(f + 1) * 64, (f // 2) * 128:(f // 2) * 128 + 128]
            turned = pltpu.roll(block, 64, 1)
            low, high = (block, turned) if f % 2 == 0 else (turned, block)
            folded = jnp.where(lane < 64, low[:32], high[32:])
            fbuf[t, f] = folded
            sbuf[t, f] = folded.astype(BF)
        for d in (2, 1, 3):
            y_copy(t, d).start()

        @pl.when(t >= LAG)
        def _():
            send_on(t - LAG)

        return carry

    lax.fori_loop(0, STEPS, step, 0)
    for t in range(STEPS - LAG, STEPS - 1):
        send_on(t)
    total = gather_y(STEPS - 1)

    def add(t, acc):
        z_copy(t).wait_recv()
        return acc + rbuf2[t]

    total = lax.fori_loop(0, STEPS - 1, add, total) * F32(scale)
    seg = (lax.broadcasted_iota(jnp.int32, (8, 128), 1) // 16) % 4
    for l in range(LEAVES):
        res = jnp.zeros((8, 128), F32)
        for q in range(4):
            moved = total[8 * q:8 * q + 8]
            shift = ((q - l) * 16) % 128
            if shift:
                moved = pltpu.roll(moved, shift, 1)
            res = jnp.where(seg == q, moved, res)
        out[l] = res

    for i, d in enumerate(order):
        if d:
            quarter_copy(i, d).wait_send()
            gather_copy(d).wait_send()

    def drain(t, carry):
        for d in range(1, NY):
            y_copy(t, d).wait_send()

        @pl.when(t < STEPS - 1)
        def _():
            z_copy(t).wait_send()

        return carry

    lax.fori_loop(0, STEPS, drain, 0)


def local(scale, grads, projection, bins, leaf):
    rows = grads.shape[0]
    quarter = rows // NO
    any_spec = pl.BlockSpec(memory_space=pl.ANY)
    dma = pltpu.SemaphoreType.DMA
    result = pl.pallas_call(
        functools.partial(kernel, scale),
        out_shape=jax.ShapeDtypeStruct((LEAVES, SK, BINS), F32),
        in_specs=[any_spec] * 4,
        out_specs=pl.BlockSpec(memory_space=pltpu.VMEM),
        scratch_shapes=[
            pltpu.VMEM((NO, quarter, grads.shape[1]), BF),
            pltpu.VMEM(projection.shape, BF),
            pltpu.VMEM((rows, 128), jnp.int32),
            pltpu.VMEM((rows // 128, 128), jnp.int32),
            pltpu.VMEM((NO, SK, quarter), F32),
            pltpu.VMEM((NO - 1, SK, quarter), F32),
            pltpu.VMEM((2 * SK, quarter // 2), BF),
            pltpu.VMEM((NO - 1, 2 * SK, quarter // 2), BF),
            pltpu.VMEM((2 * SK, rows), BF),
            pltpu.VMEM((64, rows), F32),
            pltpu.VMEM((64, rows), F32),
            pltpu.VMEM((STEPS, NY, 32, 128), F32),
            pltpu.VMEM((STEPS, NY, 32, 128), BF),
            pltpu.VMEM((STEPS, NY - 1, 32, 128), BF),
            pltpu.VMEM((STEPS - 1, 32, 128), F32),
            pltpu.VMEM((STEPS - 1, 32, 128), F32),
            dma((10,)), dma,
            dma((NO - 1,)), dma((NO - 1,)), dma((NO - 1,)), dma((NO - 1,)),
            dma((STEPS, NY - 1)), dma((STEPS, NY - 1)), dma((STEPS - 1,)), dma((STEPS - 1,)),
        ],
        compiler_params=pltpu.CompilerParams(
            collective_id=0, has_side_effects=True, vmem_limit_bytes=60 << 20
        ),
        name="sketch_histogram",
    )(grads, projection, bins, leaf.reshape(rows // 128, 128))
    return result.reshape(1, 1, LEAVES, SK, BINS)


def solution(mesh):
    placed = (P("rows", "outs"), P(), P("rows", None), P("rows"))

    def whole(grads, projection, bins, leaf):
        scale = math.sqrt(LEAVES * BINS / grads.shape[0])
        return jax.shard_map(
            functools.partial(local, scale),
            mesh=mesh,
            in_specs=placed,
            out_specs=P("rows", "outs", None, None, None),
            check_vma=False,
        )(grads, projection, bins, leaf)

    return whole
```

```python
import functools
import math

import jax
import jax.numpy as jnp
from jax import lax
from jax.experimental import pallas as pl
from jax.experimental.pallas import tpu as pltpu
from jax.sharding import PartitionSpec as P

SK = 8
BINS = 128
LEAVES = 4
MESH = pl.DeviceIdType.MESH
BF = jnp.bfloat16
F32 = jnp.float32
NX, NZ, NY, NO = 2, 8, 4, 4
STEPS = NX * NZ
PAIRS = STEPS // NX
OPEN = 2
LAG = 3


def pieces(n_rows):
    r = lax.axis_index("rows")
    return r // (NZ * NY), (r // NY) % NZ, r % NY


def kernel(
    scale,
    grads, proj, bins, leaf,
    out,
    gbuf, pbuf, bbuf, lbuf, part, skin, skq, skr, sk16, bh, cc,
    fbuf, sbuf, rbuf1, s2, rbuf2,
    lsem, ready, go, qs_send, qs_recv, ag_send, ag_recv, y_send, y_recv, z_send, z_recv,
):
    x, z, y = pieces(NX * NZ * NY)
    o = lax.axis_index("outs")
    rows = bh.shape[1]
    quarter = rows // NO
    half = quarter // 2
    order = (2, 1, 3, 0)

    pcopy = pltpu.make_async_copy(proj, pbuf, lsem.at[8])
    pcopy.start()
    gcopies = []
    for i, d in enumerate(order):
        q = (o + d) % NO
        g = pltpu.make_async_copy(
            grads.at[pl.ds(pl.multiple_of(q * quarter, quarter), quarter), :], gbuf.at[i], lsem.at[i]
        )
        g.start()
        gcopies.append(g)
    lcopy = pltpu.make_async_copy(leaf, lbuf, lsem.at[9])
    lcopy.start()
    bcopies = []
    for i in range(4):
        b = pltpu.make_async_copy(
            bins.at[pl.ds(i * quarter, quarter), pl.ds(pl.multiple_of((o // 2) * 128, 128), 128)],
            bbuf.at[pl.ds(i * quarter, quarter), :],
            lsem.at[4 + i],
        )
        bcopies.append(b)

    def row_id(xx, zz, yy):
        return xx * (NZ * NY) + zz * NY + yy

    def group(t):
        return (x + 1 - t % 2) % NX, (z + 1 + t // 2) % NZ

    here = row_id(x, z, y)
    barrier = pltpu.get_barrier_semaphore()
    leads = o == 0
    for d in range(1, NO):
        @pl.when((o + d) % NO != 0)
        def _(d=d):
            pl.semaphore_signal(barrier, inc=1, device_id=(here, (o + d) % NO), device_id_type=MESH)

    pcopy.wait()
    pmat = pbuf[:, pl.ds(pl.multiple_of(o * 256, 256), 256)]

    def quarter_copy(i, d):
        return pltpu.make_async_remote_copy(
            src_ref=part.at[i], dst_ref=skin.at[d - 1], send_sem=qs_send.at[d - 1], recv_sem=qs_recv.at[d - 1],
            device_id=(here, (o + d) % NO), device_id_type=MESH,
        )

    for i, d in enumerate(order):
        gcopies[i].wait()
        if i == 1:
            for b in bcopies:
                b.start()
        part[i] = lax.dot_general(pmat, gbuf[i], (((1,), (1,)), ((), ())), preferred_element_type=F32)
        if i == 0:
            @pl.when(jnp.logical_not(leads))
            def _():
                pl.semaphore_wait(barrier, NO - 1)
                pl.semaphore_signal(ready, inc=1, device_id=(here, 0), device_id_type=MESH)

            @pl.when(leads)
            def _():
                pl.semaphore_wait(ready, NO - 1)
                for d in range(1, NY):
                    pl.semaphore_signal(
                        barrier, inc=1, device_id=(row_id(x, z, (y + d) % NY), 0), device_id_type=MESH
                    )

                def greet(t, carry):
                    pl.semaphore_signal(barrier, inc=1, device_id=(row_id(*group(t), y), 0), device_id_type=MESH)
                    return carry

                lax.fori_loop(0, STEPS - 1, greet, 0)

        if d:
            quarter_copy(i, d).start()

    lcopy.wait()
    own_col = lax.broadcasted_iota(jnp.int32, (64, 128), 1) - (o % 2) * 64
    pick = (own_col == lax.broadcasted_iota(jnp.int32, (64, 128), 0)).astype(F32).astype(BF)

    def turn(i):
        bcopies[i].wait()
        block = bbuf[pl.ds(i * quarter, quarter), :].astype(F32).astype(BF)
        b = lax.dot_general(pick, block, (((1,), (1,)), ((), ())), preferred_element_type=F32)
        high = jnp.floor(b * F32(1.0 / 16.0))
        low = b - high * F32(16.0)
        lanes = pl.ds(i * quarter, quarter)
        bh[:, lanes] = high
        tiles = quarter // 128
        for t in range(tiles):
            leaf_row = lbuf[pl.ds(i * tiles + t, 1), :].astype(F32) * F32(16.0)
            cc[:, pl.ds(i * quarter + t * 128, 128)] = low[:, t * 128:(t + 1) * 128] + leaf_row

    turn(0)
    turn(1)
    for d in range(1, NO):
        quarter_copy(0, d).wait_recv()
    mine = ((part[3] + skin[0]) + (skin[1] + skin[2]))
    skq[...] = jnp.concatenate([mine[:, :half], mine[:, half:]], 0).astype(BF)

    def gather_copy(d):
        return pltpu.make_async_remote_copy(
            src_ref=skq, dst_ref=skr.at[d - 1], send_sem=ag_send.at[d - 1], recv_sem=ag_recv.at[d - 1],
            device_id=(here, (o + d) % NO), device_id_type=MESH,
        )

    for d in (2, 1, 3):
        gather_copy(d).start()
    turn(2)
    turn(3)

    def spread(packed, owner):
        wide = packed.astype(F32)
        for h in range(2):
            rows8 = wide[8 * h:8 * h + 8]
            sk16[:, pl.ds(pl.multiple_of(owner * quarter + h * half, half), half)] = jnp.concatenate(
                [rows8, rows8], 0
            ).astype(BF)

    spread(skq[...], o)
    for d in range(1, NO):
        gather_copy(d).wait_recv()
        spread(skr[d - 1], (o + NO - d) % NO)

    sub16 = lax.broadcasted_iota(jnp.int32, (16, rows), 0)
    pair = (sub16 // 8).astype(F32).astype(BF)
    sixteen = sub16.astype(F32).astype(BF)
    lane = lax.broadcasted_iota(jnp.int32, (32, 128), 1)

    def y_copy(i, d):
        to = (y + d) % NY
        return pltpu.make_async_remote_copy(
            src_ref=sbuf.at[i, to], dst_ref=rbuf1.at[i, d - 1], send_sem=y_send.at[i, d - 1],
            recv_sem=y_recv.at[i, d - 1], device_id=(row_id(x, z, to), o), device_id_type=MESH,
        )

    def z_copy(t):
        return pltpu.make_async_remote_copy(
            src_ref=s2.at[t], dst_ref=rbuf2.at[t], send_sem=z_send.at[t], recv_sem=z_recv.at[t],
            device_id=(row_id(*group(t), y), o), device_id_type=MESH,
        )

    def send_y(i):
        for d in (2, 1, 3):
            y_copy(i, d).start()

    def gather_y(i):
        for d in range(1, NY):
            y_copy(i, d).wait_recv()
        return [
            (fbuf[i, y, u] + rbuf1[i, 0, u].astype(F32)) + (rbuf1[i, 1, u].astype(F32) + rbuf1[i, 2, u].astype(F32))
            for u in range(NX)
        ]

    def send_on(i):
        for u, block in enumerate(gather_y(i)):
            s2[NX * i + u] = block
            z_copy(NX * i + u).start()

    def histogram(i, u):
        base = row_id(*group(NX * i + u), 0)
        weights = sk16[...]
        left, right = [], []
        for f in range(NY):
            b16 = jnp.broadcast_to(bh[pl.ds(base + f, 1), :], (16, rows)).astype(BF)
            c16 = jnp.broadcast_to(cc[pl.ds(base + f, 1), :], (16, rows)).astype(BF)
            for m in range(4):
                left.append(jnp.where(b16 == pair + BF(2 * m), weights, BF(0)))
            for m in range(4):
                right.append(jnp.where(c16 == sixteen + BF(16 * m), BF(1), BF(0)))
        both = lax.dot_general(
            jnp.concatenate(left, 0), jnp.concatenate(right, 0), (((1,), (1,)), ((), ())),
            preferred_element_type=F32,
        )
        for f in range(NY):
            block = both[f * 64:(f + 1) * 64, (f // 2) * 128:(f // 2) * 128 + 128]
            turned = pltpu.roll(block, 64, 1)
            low, high = (block, turned) if f % 2 == 0 else (turned, block)
            folded = jnp.where(lane < 64, low[:32], high[32:])
            fbuf[i, f, u] = folded
            sbuf[i, f, u] = folded.astype(BF)

    def step(i, carry):
        for u in range(NX):
            histogram(i, u)

        @pl.when(i == OPEN)
        def _():
            @pl.when(leads)
            def _():
                pl.semaphore_wait(barrier, (NY - 1) + (STEPS - 1))
                for d in range(1, NO):
                    pl.semaphore_signal(go, inc=1, device_id=(here, d), device_id_type=MESH)

            @pl.when(jnp.logical_not(leads))
            def _():
                pl.semaphore_wait(go, 1)

            for early in range(OPEN):
                send_y(early)

        @pl.when(i >= OPEN)
        def _():
            send_y(i)

        @pl.when(i >= LAG)
        def _():
            send_on(i - LAG)

        return carry

    lax.fori_loop(0, PAIRS, step, 0)
    for i in range(PAIRS - LAG, PAIRS - 1):
        send_on(i)
    other, total = gather_y(PAIRS - 1)
    s2[STEPS - 2] = other
    z_copy(STEPS - 2).start()

    def add(t, acc):
        z_copy(t).wait_recv()
        return acc + rbuf2[t]

    total = lax.fori_loop(0, STEPS - 1, add, total) * F32(scale)
    seg = (lax.broadcasted_iota(jnp.int32, (8, 128), 1) // 16) % 4
    for l in range(LEAVES):
        res = jnp.zeros((8, 128), F32)
        for q in range(4):
            moved = total[8 * q:8 * q + 8]
            shift = ((q - l) * 16) % 128
            if shift:
                moved = pltpu.roll(moved, shift, 1)
            res = jnp.where(seg == q, moved, res)
        out[l] = res

    for i, d in enumerate(order):
        if d:
            quarter_copy(i, d).wait_send()
            gather_copy(d).wait_send()

    def drain_y(i, carry):
        for d in range(1, NY):
            y_copy(i, d).wait_send()
        return carry

    def drain_z(t, carry):
        z_copy(t).wait_send()
        return carry

    lax.fori_loop(0, PAIRS, drain_y, 0)
    lax.fori_loop(0, STEPS - 1, drain_z, 0)


def local(scale, grads, projection, bins, leaf):
    rows = grads.shape[0]
    quarter = rows // NO
    any_spec = pl.BlockSpec(memory_space=pl.ANY)
    dma = pltpu.SemaphoreType.DMA
    result = pl.pallas_call(
        functools.partial(kernel, scale),
        out_shape=jax.ShapeDtypeStruct((LEAVES, SK, BINS), F32),
        in_specs=[any_spec] * 4,
        out_specs=pl.BlockSpec(memory_space=pltpu.VMEM),
        scratch_shapes=[
            pltpu.VMEM((NO, quarter, grads.shape[1]), BF),
            pltpu.VMEM(projection.shape[::-1], BF),
            pltpu.VMEM((rows, 128), jnp.int32),
            pltpu.VMEM((rows // 128, 128), jnp.int32),
            pltpu.VMEM((NO, SK, quarter), F32),
            pltpu.VMEM((NO - 1, SK, quarter), F32),
            pltpu.VMEM((2 * SK, quarter // 2), BF),
            pltpu.VMEM((NO - 1, 2 * SK, quarter // 2), BF),
            pltpu.VMEM((2 * SK, rows), BF),
            pltpu.VMEM((64, rows), F32),
            pltpu.VMEM((64, rows), F32),
            pltpu.VMEM((PAIRS, NY, NX, 32, 128), F32),
            pltpu.VMEM((PAIRS, NY, NX, 32, 128), BF),
            pltpu.VMEM((PAIRS, NY - 1, NX, 32, 128), BF),
            pltpu.VMEM((STEPS - 1, 32, 128), F32),
            pltpu.VMEM((STEPS - 1, 32, 128), F32),
            dma((10,)), pltpu.SemaphoreType.REGULAR, pltpu.SemaphoreType.REGULAR,
            dma((NO - 1,)), dma((NO - 1,)), dma((NO - 1,)), dma((NO - 1,)),
            dma((PAIRS, NY - 1)), dma((PAIRS, NY - 1)), dma((STEPS - 1,)), dma((STEPS - 1,)),
        ],
        compiler_params=pltpu.CompilerParams(
            collective_id=0, has_side_effects=True, vmem_limit_bytes=60 << 20
        ),
        name="sketch_histogram",
    )(grads, projection.T, bins, leaf.reshape(rows // 128, 128))
    return result.reshape(1, 1, LEAVES, SK, BINS)


def solution(mesh):
    placed = (P("rows", "outs"), P(), P("rows", None), P("rows"))

    def whole(grads, projection, bins, leaf):
        scale = math.sqrt(LEAVES * BINS / grads.shape[0])
        return jax.shard_map(
            functools.partial(local, scale),
            mesh=mesh,
            in_specs=placed,
            out_specs=P("rows", "outs", None, None, None),
            check_vma=False,
        )(grads, projection, bins, leaf)

    return whole
```

```python
import functools
import math

import jax
import jax.numpy as jnp
from jax import lax
from jax.experimental import pallas as pl
from jax.experimental.pallas import tpu as pltpu
from jax.sharding import PartitionSpec as P

SK = 8
BINS = 128
LEAVES = 4
MESH = pl.DeviceIdType.MESH
BF = jnp.bfloat16
F32 = jnp.float32
NX, NZ, NY, NO = 2, 8, 4, 4
STEPS = NX * NZ
ROUNDS = STEPS // NX
BATCHES = ((0, 4), (4, 4), (8, 4), (12, 2), (14, 2))
DEPTH = 256


def pieces(n_rows):
    r = lax.axis_index("rows")
    return r // (NZ * NY), (r // NY) % NZ, r % NY


def kernel(
    scale,
    grads, proj, bins, leaf,
    out,
    gbuf, pbuf, bbuf, lbuf, part, skin, skq, skr, sk16, bh, cc,
    fbuf, sbuf, rbuf1, s2, rbuf2,
    lsem, ready, go, qs_send, qs_recv, ag_send, ag_recv, y_send, y_recv, z_send, z_recv,
):
    x, z, y = pieces(NX * NZ * NY)
    o = lax.axis_index("outs")
    rows = bh.shape[1]
    quarter = rows // NO
    half = quarter // 2
    order = (2, 1, 3, 0)

    pcopy = pltpu.make_async_copy(proj, pbuf, lsem.at[8])
    pcopy.start()
    gcopies = []
    for i, d in enumerate(order):
        q = (o + d) % NO
        g = pltpu.make_async_copy(
            grads.at[pl.ds(pl.multiple_of(q * quarter, quarter), quarter), :], gbuf.at[i], lsem.at[i]
        )
        g.start()
        gcopies.append(g)
    lcopy = pltpu.make_async_copy(leaf, lbuf, lsem.at[9])
    lcopy.start()
    bcopies = []
    for i in range(4):
        b = pltpu.make_async_copy(
            bins.at[pl.ds(i * quarter, quarter), pl.ds(pl.multiple_of((o // 2) * 128, 128), 128)],
            bbuf.at[pl.ds(i * quarter, quarter), :],
            lsem.at[4 + i],
        )
        bcopies.append(b)

    def row_id(xx, zz, yy):
        return xx * (NZ * NY) + zz * NY + yy

    def group(t):
        w = t - 7 * (t // 8)
        return (x + w + (w % 8) // 6) % NX, ((z // 4 + 1 - t // 8) % 2) * 4 + (z % 4 + w // 2) % 4

    here = row_id(x, z, y)
    barrier = pltpu.get_barrier_semaphore()
    leads = o == 0
    for d in range(1, NO):
        @pl.when((o + d) % NO != 0)
        def _(d=d):
            pl.semaphore_signal(barrier, inc=1, device_id=(here, (o + d) % NO), device_id_type=MESH)

    pcopy.wait()
    wide = pbuf[:, pl.ds(pl.multiple_of(o * 256, 256), 256)].astype(F32)
    pmat = jnp.concatenate([wide, wide], 0).astype(BF)

    def multiply(left, rights, take):
        def body(*accs):
            for n, right in enumerate(rights):
                pltpu.matmul_push_rhs(right, (n // 2) % 2, n % 2, transpose=True)
                pltpu.matmul_acc_lhs(accs[n], left, load_staged_rhs=(n // 2) % 2)
            for n in range(len(rights)):
                take(n, pltpu.matmul_pop(accs[n]))

        pl.run_scoped(body, *(pltpu.ACC(n % 2)((left.shape[0], DEPTH), F32) for n in range(len(rights))))

    def put_part(i, n, value):
        part[i, :, pl.ds(n * DEPTH, DEPTH)] = value[:SK]

    def quarter_copy(i, d):
        return pltpu.make_async_remote_copy(
            src_ref=part.at[i], dst_ref=skin.at[d - 1], send_sem=qs_send, recv_sem=qs_recv,
            device_id=(here, (o + d) % NO), device_id_type=MESH,
        )

    def enter():
        @pl.when(jnp.logical_not(leads))
        def _():
            pl.semaphore_wait(barrier, NO - 1)
            pl.semaphore_signal(ready, inc=1, device_id=(here, 0), device_id_type=MESH)

        @pl.when(leads)
        def _():
            pl.semaphore_wait(ready, NO - 1)

    for i, d in enumerate(order):
        gcopies[i].wait()
        if i == 1:
            for b in bcopies:
                b.start()
        multiply(
            pmat, [gbuf[i, pl.ds(n * DEPTH, DEPTH), :] for n in range(quarter // DEPTH)],
            lambda n, value: put_part(i, n, value),
        )
        if i == 0:
            enter()
        if d:
            quarter_copy(i, d).start()

    @pl.when(leads)
    def _():
        for d in range(1, NY):
            pl.semaphore_signal(
                barrier, inc=1, device_id=(row_id(x, z, (y + d) % NY), 0), device_id_type=MESH
            )

        def greet(t, carry):
            pl.semaphore_signal(barrier, inc=1, device_id=(row_id(*group(t), y), 0), device_id_type=MESH)
            return carry

        lax.fori_loop(0, STEPS - 1, greet, 0)

    lcopy.wait()
    row_at = lax.broadcasted_iota(jnp.int32, (128, 256), 0)
    col_at = lax.broadcasted_iota(jnp.int32, (128, 256), 1)
    wanted = (row_at // 64) * 128 + (o % 2) * 64 + row_at % 64
    pick = (col_at == wanted).astype(F32).astype(BF)
    per_row = 128

    def put_bins(i, n, value):
        for h in range(2):
            b = value[64 * h:64 * h + 64]
            high = jnp.floor(b * F32(1.0 / 16.0))
            low = b - high * F32(16.0)
            at = i * quarter + (2 * n + h) * DEPTH
            bh[:, pl.ds(at, DEPTH)] = high
            for t in range(DEPTH // per_row):
                leaf_row = lbuf[pl.ds(at // per_row + t, 1), :].astype(F32) * F32(16.0)
                cc[:, pl.ds(at + t * per_row, per_row)] = low[:, t * per_row:(t + 1) * per_row] + leaf_row

    def turn(i):
        bcopies[i].wait()
        blocks = [
            bbuf[pl.ds(i * quarter + n * DEPTH, DEPTH), :].astype(F32).astype(BF) for n in range(quarter // DEPTH)
        ]
        multiply(
            pick, [jnp.concatenate(blocks[n:n + 2], 1) for n in range(0, len(blocks), 2)],
            lambda n, value: put_bins(i, n, value),
        )

    turn(0)
    turn(1)
    pltpu.make_async_copy(skin, skin, qs_recv).wait()
    mine = ((part[3] + skin[0]) + (skin[1] + skin[2]))
    skq[...] = jnp.concatenate([mine[:, :half], mine[:, half:]], 0).astype(BF)

    def gather_copy(d):
        return pltpu.make_async_remote_copy(
            src_ref=skq, dst_ref=skr.at[d - 1], send_sem=ag_send, recv_sem=ag_recv,
            device_id=(here, (o + d) % NO), device_id_type=MESH,
        )

    for d in (2, 1, 3):
        gather_copy(d).start()
    turn(2)
    turn(3)

    def spread(packed, owner):
        wide = packed.astype(F32)
        for h in range(2):
            rows8 = wide[8 * h:8 * h + 8]
            sk16[:, pl.ds(pl.multiple_of(owner * quarter + h * half, half), half)] = jnp.concatenate(
                [rows8, rows8], 0
            ).astype(BF)

    spread(skq[...], o)
    pltpu.make_async_copy(skr, skr, ag_recv).wait()
    for d in range(1, NO):
        spread(skr[d - 1], (o + NO - d) % NO)

    sub16 = lax.broadcasted_iota(jnp.int32, (16, DEPTH), 0)
    pair = (sub16 // 8).astype(F32).astype(BF)
    sixteen = sub16.astype(F32).astype(BF)
    lane = lax.broadcasted_iota(jnp.int32, (32, 128), 1)

    def y_copy(b, d):
        to, (first, n) = (y + d) % NY, BATCHES[b]
        return pltpu.make_async_remote_copy(
            src_ref=sbuf.at[to, pl.ds(first, n)], dst_ref=rbuf1.at[d - 1, pl.ds(first, n)], send_sem=y_send,
            recv_sem=y_recv.at[b], device_id=(row_id(x, z, to), o), device_id_type=MESH,
        )

    def z_copy(t):
        return pltpu.make_async_remote_copy(
            src_ref=s2.at[t], dst_ref=rbuf2.at[t], send_sem=z_send, recv_sem=z_recv,
            device_id=(row_id(*group(t), y), o), device_id_type=MESH,
        )

    def send_y(b):
        for d in (2, 1, 3):
            y_copy(b, d).start()

    def gather_y(b):
        first, n = BATCHES[b]
        came = rbuf1.at[:, pl.ds(first, n)]
        pltpu.make_async_copy(came, came, y_recv.at[b]).wait()
        return [
            (fbuf[y, t] + rbuf1[0, t].astype(F32)) + (rbuf1[1, t].astype(F32) + rbuf1[2, t].astype(F32))
            for t in range(first, first + n)
        ]

    def send_on(b):
        for t, block in enumerate(gather_y(b), BATCHES[b][0]):
            s2[t] = block
            z_copy(t).start()

    def feed(acc, unit, base, k, slot):
        lanes = pl.ds(k * DEPTH, DEPTH)
        weights = sk16[:, lanes]
        left, right = [], []
        for f in range(NY):
            b16 = jnp.broadcast_to(bh[pl.ds(base + f, 1), lanes], (16, DEPTH)).astype(BF)
            c16 = jnp.broadcast_to(cc[pl.ds(base + f, 1), lanes], (16, DEPTH)).astype(BF)
            for m in range(4):
                left.append(jnp.where(b16 == pair + BF(2 * m), weights, BF(0)))
                right.append(jnp.where(c16 == sixteen + BF(16 * m), BF(1), BF(0)))
        pltpu.matmul_push_rhs(jnp.concatenate(right, 0), slot, unit, transpose=True)
        pltpu.matmul_acc_lhs(acc, jnp.concatenate(left, 0), load_staged_rhs=slot)

    def keep(t, both):
        for f in range(NY):
            block = both[f * 64:(f + 1) * 64, (f // 2) * 128:(f // 2) * 128 + 128]
            turned = pltpu.roll(block, 64, 1)
            low, high = (block, turned) if f % 2 == 0 else (turned, block)
            folded = jnp.where(lane < 64, low[:32], high[32:])
            fbuf[f, t] = folded
            sbuf[f, t] = folded.astype(BF)

    def with_sums(body):
        pl.run_scoped(body, *(pltpu.ACC(unit)((256, 256), F32) for unit in range(2)))

    def two_groups(i):
        bases = [row_id(*group(NX * i + u), 0) for u in range(NX)]

        def body(*sums):
            for k in range(rows // DEPTH):
                for u in range(NX):
                    feed(sums[u], u, bases[u], k, k % 2)
            for u in range(NX):
                keep(NX * i + u, pltpu.matmul_pop(sums[u]))

        with_sums(body)

    late = z // (NZ // 2) == 1

    def open_sends():
        @pl.when(leads)
        def _():
            pl.semaphore_wait(barrier, (NY - 1) + (STEPS - 1))
            for d in range(1, NO):
                pl.semaphore_signal(go, inc=1, device_id=(here, d), device_id_type=MESH)

        @pl.when(jnp.logical_not(leads))
        def _():
            pl.semaphore_wait(go, 1)

        send_y(0)

    def step(i, carry):
        two_groups(i)

        @pl.when(jnp.logical_and(i == 1, late))
        def _():
            open_sends()

        @pl.when(i == 3)
        def _():
            @pl.when(jnp.logical_not(late))
            def _():
                open_sends()

            send_y(1)

            @pl.when(late)
            def _():
                send_on(0)

        @pl.when(i == 5)
        def _():
            send_y(2)

            @pl.when(jnp.logical_not(late))
            def _():
                send_on(0)

            send_on(1)

        @pl.when(i == 6)
        def _():
            send_y(3)
            send_on(2)

        return carry

    lax.fori_loop(0, ROUNDS, step, 0)
    send_y(4)
    send_on(3)
    near, total = gather_y(4)
    s2[STEPS - 2] = near
    z_copy(STEPS - 2).start()
    pltpu.make_async_copy(rbuf2, rbuf2, z_recv).wait()
    for t in range(STEPS - 1):
        total = total + rbuf2[t]
    total = total * F32(scale)
    seg = (lax.broadcasted_iota(jnp.int32, (8, 128), 1) // 16) % 4
    for l in range(LEAVES):
        res = jnp.zeros((8, 128), F32)
        for q in range(4):
            moved = total[8 * q:8 * q + 8]
            shift = ((q - l) * 16) % 128
            if shift:
                moved = pltpu.roll(moved, shift, 1)
            res = jnp.where(seg == q, moved, res)
        out[l] = res

    pltpu.make_async_copy(skin, skin, qs_send).wait()
    pltpu.make_async_copy(skr, skr, ag_send).wait()
    pltpu.make_async_copy(rbuf1, rbuf1, y_send).wait()
    pltpu.make_async_copy(rbuf2, rbuf2, z_send).wait()


def local(scale, grads, projection, bins, leaf):
    rows = grads.shape[0]
    quarter = rows // NO
    any_spec = pl.BlockSpec(memory_space=pl.ANY)
    dma = pltpu.SemaphoreType.DMA
    result = pl.pallas_call(
        functools.partial(kernel, scale),
        out_shape=jax.ShapeDtypeStruct((LEAVES, SK, BINS), F32),
        in_specs=[any_spec] * 4,
        out_specs=pl.BlockSpec(memory_space=pltpu.VMEM),
        scratch_shapes=[
            pltpu.VMEM((NO, quarter, grads.shape[1]), BF),
            pltpu.VMEM(projection.shape[::-1], BF),
            pltpu.VMEM((rows, 128), jnp.int32),
            pltpu.VMEM((rows // 128, 128), jnp.int32),
            pltpu.VMEM((NO, SK, quarter), F32),
            pltpu.VMEM((NO - 1, SK, quarter), F32),
            pltpu.VMEM((2 * SK, quarter // 2), BF),
            pltpu.VMEM((NO - 1, 2 * SK, quarter // 2), BF),
            pltpu.VMEM((2 * SK, rows), BF),
            pltpu.VMEM((64, rows), F32),
            pltpu.VMEM((64, rows), F32),
            pltpu.VMEM((NY, STEPS, 32, 128), F32),
            pltpu.VMEM((NY, STEPS, 32, 128), BF),
            pltpu.VMEM((NY - 1, STEPS, 32, 128), BF),
            pltpu.VMEM((STEPS - 1, 32, 128), F32),
            pltpu.VMEM((STEPS - 1, 32, 128), F32),
            dma((10,)), pltpu.SemaphoreType.REGULAR, pltpu.SemaphoreType.REGULAR,
            dma, dma, dma, dma, dma, dma((len(BATCHES),)), dma, dma,
        ],
        compiler_params=pltpu.CompilerParams(
            collective_id=0, has_side_effects=True, vmem_limit_bytes=54 << 20
        ),
        name="sketch_histogram",
    )(grads, projection.T, bins, leaf.reshape(rows // 128, 128))
    return result.reshape(1, 1, LEAVES, SK, BINS)


def solution(mesh):
    placed = (P("rows", "outs"), P(), P("rows", None), P("rows"))

    def whole(grads, projection, bins, leaf):
        scale = math.sqrt(LEAVES * BINS / grads.shape[0])
        return jax.shard_map(
            functools.partial(local, scale),
            mesh=mesh,
            in_specs=placed,
            out_specs=P("rows", "outs", None, None, None),
            check_vma=False,
        )(grads, projection, bins, leaf)

    return whole
```

```python
import functools
import math

import jax
import jax.numpy as jnp
from jax import lax
from jax.experimental import pallas as pl
from jax.experimental.pallas import tpu as pltpu
from jax.sharding import PartitionSpec as P

SK = 8
BINS = 128
LEAVES = 4
MESH = pl.DeviceIdType.MESH
BF = jnp.bfloat16
F32 = jnp.float32
NX, NZ, NY, NO = 2, 8, 4, 4
STEPS = NX * NZ
ROUNDS = STEPS // NX
BATCHES = ((0, 4), (4, 4), (8, 4), (12, 2), (14, 2))
DEPTH = 256


def pieces(n_rows):
    r = lax.axis_index("rows")
    return r // (NZ * NY), (r // NY) % NZ, r % NY


def kernel(
    scale,
    grads, proj, bins, leaf,
    out,
    gbuf, pbuf, bbuf, lbuf, part, skin, skq, skr, sk16, bh, cc,
    fbuf, sbuf, rbuf1, s2, rbuf2,
    lsem, ready, go, qs_send, qs_recv, ag_send, ag_recv, y_send, y_recv, z_send, z_recv,
):
    x, z, y = pieces(NX * NZ * NY)
    o = lax.axis_index("outs")
    rows = bh.shape[1]
    quarter = rows // NO
    half = quarter // 2
    order = (2, 1, 3, 0)

    pcopy = pltpu.make_async_copy(proj, pbuf, lsem.at[8])
    pcopy.start()
    gcopies = []
    for i, d in enumerate(order):
        q = (o + d) % NO
        g = pltpu.make_async_copy(
            grads.at[pl.ds(pl.multiple_of(q * quarter, quarter), quarter), :], gbuf.at[i], lsem.at[i]
        )
        g.start()
        gcopies.append(g)
    lcopy = pltpu.make_async_copy(leaf, lbuf, lsem.at[9])
    lcopy.start()
    bcopies = []
    for i in range(4):
        b = pltpu.make_async_copy(
            bins.at[pl.ds(i * quarter, quarter), pl.ds(pl.multiple_of((o // 2) * 128, 128), 128)],
            bbuf.at[pl.ds(i * quarter, quarter), :],
            lsem.at[4 + i],
        )
        bcopies.append(b)

    def row_id(xx, zz, yy):
        return xx * (NZ * NY) + zz * NY + yy

    def group(t):
        w = t - 7 * (t // 8)
        return (x + w + (w % 8) // 6) % NX, ((z // 4 + 1 - t // 8) % 2) * 4 + (z % 4 + w // 2) % 4

    here = row_id(x, z, y)
    barrier = pltpu.get_barrier_semaphore()
    leads = o == 0
    for d in range(1, NO):
        @pl.when((o + d) % NO != 0)
        def _(d=d):
            pl.semaphore_signal(barrier, inc=1, device_id=(here, (o + d) % NO), device_id_type=MESH)

    pcopy.wait()
    wide = pbuf[:, pl.ds(pl.multiple_of(o * 256, 256), 256)].astype(F32)
    pmat = jnp.concatenate([wide, wide], 0).astype(BF)

    def multiply(left, rights, take):
        def body(*accs):
            for n, right in enumerate(rights):
                pltpu.matmul_push_rhs(right, (n // 2) % 2, n % 2, transpose=True)
                pltpu.matmul_acc_lhs(accs[n], left, load_staged_rhs=(n // 2) % 2)
            for n in range(len(rights)):
                take(n, pltpu.matmul_pop(accs[n]))

        pl.run_scoped(body, *(pltpu.ACC(n % 2)((left.shape[0], DEPTH), F32) for n in range(len(rights))))

    def put_part(i, n, value):
        part[i, :, pl.ds(n * DEPTH, DEPTH)] = value[:SK]

    def quarter_copy(i, d):
        return pltpu.make_async_remote_copy(
            src_ref=part.at[i], dst_ref=skin.at[d - 1], send_sem=qs_send, recv_sem=qs_recv,
            device_id=(here, (o + d) % NO), device_id_type=MESH,
        )

    def enter():
        @pl.when(jnp.logical_not(leads))
        def _():
            pl.semaphore_wait(barrier, NO - 1)
            pl.semaphore_signal(ready, inc=1, device_id=(here, 0), device_id_type=MESH)

        @pl.when(leads)
        def _():
            pl.semaphore_wait(ready, NO - 1)

    for i, d in enumerate(order):
        gcopies[i].wait()
        if i == 1:
            for b in bcopies:
                b.start()
        multiply(
            pmat, [gbuf[i, pl.ds(n * DEPTH, DEPTH), :] for n in range(quarter // DEPTH)],
            lambda n, value: put_part(i, n, value),
        )
        if i == 0:
            enter()
        if d:
            quarter_copy(i, d).start()

    @pl.when(leads)
    def _():
        for d in range(1, NY):
            pl.semaphore_signal(
                barrier, inc=1, device_id=(row_id(x, z, (y + d) % NY), 0), device_id_type=MESH
            )

        def greet(t, carry):
            pl.semaphore_signal(barrier, inc=1, device_id=(row_id(*group(t), y), 0), device_id_type=MESH)
            return carry

        lax.fori_loop(0, STEPS - 1, greet, 0)

    lcopy.wait()
    row_at = lax.broadcasted_iota(jnp.int32, (128, 256), 0)
    col_at = lax.broadcasted_iota(jnp.int32, (128, 256), 1)
    wanted = (row_at // 64) * 128 + (o % 2) * 64 + row_at % 64
    pick = (col_at == wanted).astype(F32).astype(BF)
    per_row = 128

    def put_bins(i, n, value):
        for h in range(2):
            b = value[64 * h:64 * h + 64]
            high = jnp.floor(b * F32(1.0 / 16.0))
            low = b - high * F32(16.0)
            at = i * quarter + (2 * n + h) * DEPTH
            bh[:, pl.ds(at, DEPTH)] = high
            for t in range(DEPTH // per_row):
                leaf_row = lbuf[pl.ds(at // per_row + t, 1), :].astype(F32) * F32(16.0)
                cc[:, pl.ds(at + t * per_row, per_row)] = low[:, t * per_row:(t + 1) * per_row] + leaf_row

    def turn(i):
        bcopies[i].wait()
        blocks = [
            bbuf[pl.ds(i * quarter + n * DEPTH, DEPTH), :].astype(F32).astype(BF) for n in range(quarter // DEPTH)
        ]
        multiply(
            pick, [jnp.concatenate(blocks[n:n + 2], 1) for n in range(0, len(blocks), 2)],
            lambda n, value: put_bins(i, n, value),
        )

    turn(0)
    turn(1)
    pltpu.make_async_copy(skin, skin, qs_recv).wait()
    mine = ((part[3] + skin[0]) + (skin[1] + skin[2]))
    skq[...] = jnp.concatenate([mine[:, :half], mine[:, half:]], 0).astype(BF)

    def gather_copy(d):
        return pltpu.make_async_remote_copy(
            src_ref=skq, dst_ref=skr.at[d - 1], send_sem=ag_send, recv_sem=ag_recv,
            device_id=(here, (o + d) % NO), device_id_type=MESH,
        )

    for d in (2, 1, 3):
        gather_copy(d).start()
    turn(2)
    turn(3)

    def spread(packed, owner):
        wide = packed.astype(F32)
        for h in range(2):
            rows8 = wide[8 * h:8 * h + 8]
            sk16[:, pl.ds(pl.multiple_of(owner * quarter + h * half, half), half)] = jnp.concatenate(
                [rows8, rows8], 0
            ).astype(BF)

    spread(skq[...], o)
    pltpu.make_async_copy(skr, skr, ag_recv).wait()
    for d in range(1, NO):
        spread(skr[d - 1], (o + NO - d) % NO)

    sub16 = lax.broadcasted_iota(jnp.int32, (16, DEPTH), 0)
    pair = (sub16 // 8).astype(F32).astype(BF)
    sixteen = sub16.astype(F32).astype(BF)
    lane = lax.broadcasted_iota(jnp.int32, (32, 128), 1)

    def y_copy(b, d):
        to, (first, n) = (y + d) % NY, BATCHES[b]
        return pltpu.make_async_remote_copy(
            src_ref=sbuf.at[to, pl.ds(first, n)], dst_ref=rbuf1.at[d - 1, pl.ds(first, n)], send_sem=y_send,
            recv_sem=y_recv.at[b], device_id=(row_id(x, z, to), o), device_id_type=MESH,
        )

    def z_copy(t):
        return pltpu.make_async_remote_copy(
            src_ref=s2.at[t], dst_ref=rbuf2.at[t], send_sem=z_send, recv_sem=z_recv,
            device_id=(row_id(*group(t), y), o), device_id_type=MESH,
        )

    def send_y(b):
        for d in (2, 1, 3):
            y_copy(b, d).start()

    def gather_y(b):
        first, n = BATCHES[b]
        came = rbuf1.at[:, pl.ds(first, n)]
        pltpu.make_async_copy(came, came, y_recv.at[b]).wait()
        return [
            (fbuf[y, t] + rbuf1[0, t].astype(F32)) + (rbuf1[1, t].astype(F32) + rbuf1[2, t].astype(F32))
            for t in range(first, first + n)
        ]

    def send_on(b):
        for t, block in enumerate(gather_y(b), BATCHES[b][0]):
            s2[t] = block
            z_copy(t).start()

    def feed(acc, unit, base, k, slot):
        lanes = pl.ds(k * DEPTH, DEPTH)
        weights = sk16[:, lanes]
        left, right = [], []
        for f in range(NY):
            b16 = jnp.broadcast_to(bh[pl.ds(base + f, 1), lanes], (16, DEPTH)).astype(BF)
            c16 = jnp.broadcast_to(cc[pl.ds(base + f, 1), lanes], (16, DEPTH)).astype(BF)
            for m in range(4):
                left.append(jnp.where(b16 == pair + BF(2 * m), weights, BF(0)))
                right.append(jnp.where(c16 == sixteen + BF(16 * m), BF(1), BF(0)))
        pltpu.matmul_push_rhs(jnp.concatenate(right, 0), slot, unit, transpose=True)
        pltpu.matmul_acc_lhs(acc, jnp.concatenate(left, 0), load_staged_rhs=slot)

    def keep(t, both):
        for f in range(NY):
            block = both[f * 64:(f + 1) * 64, (f // 2) * 128:(f // 2) * 128 + 128]
            turned = pltpu.roll(block, 64, 1)
            low, high = (block, turned) if f % 2 == 0 else (turned, block)
            folded = jnp.where(lane < 64, low[:32], high[32:])
            fbuf[f, t] = folded
            sbuf[f, t] = folded.astype(BF)

    def with_sums(body):
        pl.run_scoped(body, *(pltpu.ACC(unit)((256, 256), F32) for unit in range(2)))

    def two_groups(i):
        bases = [row_id(*group(NX * i + u), 0) for u in range(NX)]

        def body(*sums):
            for k in range(rows // DEPTH):
                for u in range(NX):
                    feed(sums[u], u, bases[u], k, k % 2)
            for u in range(NX):
                keep(NX * i + u, pltpu.matmul_pop(sums[u]))

        with_sums(body)

    late = z // (NZ // 2) == 1

    def open_sends():
        @pl.when(leads)
        def _():
            pl.semaphore_wait(barrier, (NY - 1) + (STEPS - 1))
            for d in range(1, NO):
                pl.semaphore_signal(go, inc=1, device_id=(here, d), device_id_type=MESH)

        @pl.when(jnp.logical_not(leads))
        def _():
            pl.semaphore_wait(go, 1)

        send_y(0)

    def step(i, carry):
        two_groups(i)

        @pl.when(jnp.logical_and(i == 1, late))
        def _():
            open_sends()

        @pl.when(i == 3)
        def _():
            @pl.when(jnp.logical_not(late))
            def _():
                open_sends()

            send_y(1)

            @pl.when(late)
            def _():
                send_on(0)

        @pl.when(i == 5)
        def _():
            send_y(2)

            @pl.when(jnp.logical_not(late))
            def _():
                send_on(0)

            send_on(1)

        @pl.when(i == 6)
        def _():
            send_y(3)
            send_on(2)

        return carry

    lax.fori_loop(0, ROUNDS, step, 0)
    send_y(4)
    send_on(3)
    near, total = gather_y(4)
    s2[STEPS - 2] = near
    z_copy(STEPS - 2).start()
    pltpu.make_async_copy(rbuf2, rbuf2, z_recv).wait()
    for t in range(STEPS - 1):
        total = total + rbuf2[t]
    total = total * F32(scale)
    seg = (lax.broadcasted_iota(jnp.int32, (8, 128), 1) // 16) % 4
    for l in range(LEAVES):
        res = jnp.zeros((8, 128), F32)
        for q in range(4):
            moved = total[8 * q:8 * q + 8]
            shift = ((q - l) * 16) % 128
            if shift:
                moved = pltpu.roll(moved, shift, 1)
            res = jnp.where(seg == q, moved, res)
        out[l] = res

    pltpu.make_async_copy(skin, skin, qs_send).wait()
    pltpu.make_async_copy(skr, skr, ag_send).wait()
    pltpu.make_async_copy(rbuf1, rbuf1, y_send).wait()
    pltpu.make_async_copy(rbuf2, rbuf2, z_send).wait()


def local(scale, grads, projection, bins, leaf):
    rows = grads.shape[0]
    quarter = rows // NO
    any_spec = pl.BlockSpec(memory_space=pl.ANY)
    dma = pltpu.SemaphoreType.DMA
    result = pl.pallas_call(
        functools.partial(kernel, scale),
        out_shape=jax.ShapeDtypeStruct((LEAVES, SK, BINS), F32),
        in_specs=[any_spec] * 4,
        out_specs=pl.BlockSpec(memory_space=pltpu.VMEM),
        scratch_shapes=[
            pltpu.VMEM((NO, quarter, grads.shape[1]), BF),
            pltpu.VMEM(projection.shape[::-1], BF),
            pltpu.VMEM((rows, 128), jnp.int32),
            pltpu.VMEM((rows // 128, 128), jnp.int32),
            pltpu.VMEM((NO, SK, quarter), F32),
            pltpu.VMEM((NO - 1, SK, quarter), F32),
            pltpu.VMEM((2 * SK, quarter // 2), BF),
            pltpu.VMEM((NO - 1, 2 * SK, quarter // 2), BF),
            pltpu.VMEM((2 * SK, rows), BF),
            pltpu.VMEM((64, rows), F32),
            pltpu.VMEM((64, rows), F32),
            pltpu.VMEM((NY, STEPS, 32, 128), F32),
            pltpu.VMEM((NY, STEPS, 32, 128), BF),
            pltpu.VMEM((NY - 1, STEPS, 32, 128), BF),
            pltpu.VMEM((STEPS - 1, 32, 128), F32),
            pltpu.VMEM((STEPS - 1, 32, 128), F32),
            dma((10,)), pltpu.SemaphoreType.REGULAR, pltpu.SemaphoreType.REGULAR,
            dma, dma, dma, dma, dma, dma((len(BATCHES),)), dma, dma,
        ],
        compiler_params=pltpu.CompilerParams(
            collective_id=0, has_side_effects=True, vmem_limit_bytes=55212 << 10
        ),
        name="sketch_histogram",
    )(grads, projection.T, bins, leaf.reshape(rows // 128, 128))
    return result.reshape(1, 1, LEAVES, SK, BINS)


def solution(mesh):
    placed = (P("rows", "outs"), P(), P("rows", None), P("rows"))

    def whole(grads, projection, bins, leaf):
        scale = math.sqrt(LEAVES * BINS / grads.shape[0])
        return jax.shard_map(
            functools.partial(local, scale),
            mesh=mesh,
            in_specs=placed,
            out_specs=P("rows", "outs", None, None, None),
            check_vma=False,
        )(grads, projection, bins, leaf)

    return whole
```
